32 devices in a mesh: grp: 2 (over y), space: 4 (over z), vec: 4 (over x, core).
Axes of the slice: x: 2, y: 2, z: 4, core: 2. Of those that a mesh axis runs over, the one named last changes fastest.
Arguments:
- eigvecs: bfloat16 [2, 3, 8, 2, 4, 32, 512], P(None, None, ('grp', 'space')), parts along dimension 2, may hold values from -6 to 6
- links: bfloat16 [3, 2, 3, 3, 8, 2, 4, 32], P(None, None, None, None, ('grp', 'space')), parts along dimension 4, may hold values from -2.5 to 2.5
- momenta: int32 [2, 3], replicated, may hold values from -2 to 2
- direction: int32 [3], replicated, may hold values from 1 to 3
- perambulator: bfloat16 [2, 4, 64, 512], P(None, None, ('grp', 'space')), parts along dimension 2, may hold values from -0.1875 to 0.1875
- column_momentum: int32 [64], P(('grp', 'space')), parts along dimension 0, may hold values from 0 to 1
Outputs:
- elementals: float32 [1024, 2, 2, 512], P(('grp', 'space'), None, None, 'vec'), parts along dimension 0
- mixed_out: float32 [2, 4, 64, 512], P(None, None, ('grp', 'space'), 'vec'), parts along dimension 2
The draws below stay inside these ranges and needn't reach their ends.
There are 2 independent parts, one for each index of `grp`. The reference program is written for one: setup_inputs(seed, part) draws one part's arguments, and reference() takes and returns one part's arrays. A program takes and returns all parts, laid end to end along the dimension named above; an argument that names none is the same for every part. Nothing has to cross between parts.
Inputs may be any that keep to these rules, and one draw needn't show every extreme that they name: `direction`: every component nonzero.
All inputs are finite; a program needn't handle non-finite values.
Results may differ from the reference program's by a relative error of at most 0.0049.
Values may be sent and summed in bfloat16 or wider, within the bound.
No kernel may reach another device: no remote copies, remote signals or barrier semaphores. Data moves between devices by JAX's collectives and lax.ppermute only.
A program may use at most 64 MiB of HBM per device.

```python
import math
import jax
import jax.numpy as jnp
from jax import lax

NEV = 512
MOM = 2
LX = 32
YSPLIT = 4
CY = 4
CZ = 2
NZ = 2
NY = 16
NSRC = 32
N_SPACE = 4


def touch_ends(values, key, low, high):
    index_at = [jax.random.randint(jax.random.fold_in(key, axis), (), 0, length) for axis, length in enumerate(values.shape)]
    longest = values.shape.index(max(values.shape))
    neighbour = index_at[:longest] + [(index_at[longest] + 1) % values.shape[longest]] + index_at[longest + 1:]
    return values.at[tuple(index_at)].set(low).at[tuple(neighbour)].set(high)


def level_of(stream_key, dims, shards, least, top_value):
    factor_of = 1.0
    for axis_at, shards_of in shards:
        heights = jax.random.uniform(jax.random.fold_in(jax.random.fold_in(stream_key, 6), axis_at), (shards_of,), jnp.float32, least / len(shards), top_value / len(shards))
        factor_of = factor_of * jnp.repeat(jnp.exp(heights), dims[axis_at] // shards_of).reshape((-1,) + (1,) * (len(dims) - 1 - axis_at))
    return factor_of


def normal_values(own_key, extent, deviation, reach, split=(), kind=jnp.bfloat16):
    values = jax.random.normal(own_key, extent, jnp.float32) * deviation
    if len(split) > 0:
        values = level_of(own_key, extent, split, -0.22, 0.18) * values
    return jnp.clip(values, min=-reach, max=reach).astype(kind)


def setup_inputs(seed: int = 0, part: int = 0) -> dict:
    arg_keys = jax.random.split(jax.random.key(seed), 7)
    own_keys = jax.random.split(jax.random.fold_in(arg_keys[6], part), 7)
    return {
        "eigvecs": normal_values(own_keys[0], (2, 3, N_SPACE, CZ, CY, LX, NEV), 1.0, 6.0, ((2, 4),)),
        "links": normal_values(own_keys[1], (3, 2, 3, 3, N_SPACE, CZ, CY, LX), 6 ** -0.5, 2.5, ((4, 4),)),
        "momenta": touch_ends(jax.random.randint(arg_keys[2], (MOM, 3), -2, 3), jax.random.fold_in(arg_keys[2], 1), -2, 2).astype(jnp.int32),
        "direction": jax.random.randint(arg_keys[3], (3,), 1, 4).astype(jnp.int32),
        "perambulator": normal_values(own_keys[4], (2, 4, NSRC, NEV), (2 * NEV) ** -0.5, 0.1875, ((2, 4),)),
        "column_momentum": touch_ends(jax.random.randint(own_keys[5], (NSRC,), 0, MOM), jax.random.fold_in(own_keys[5], 1), 0, MOM - 1).astype(jnp.int32),
    }


def link_times(links_block, colour_field, adjoint):
    out_re = []
    out_im = []
    for colour_out in range(3):
        total_re = None
        total_im = None
        for colour_in in range(3):
            if adjoint:
                link_re = links_block[0, colour_in, colour_out][..., None]
                link_im = -links_block[1, colour_in, colour_out][..., None]
            else:
                link_re = links_block[0, colour_out, colour_in][..., None]
                link_im = links_block[1, colour_out, colour_in][..., None]
            part_re = link_re * colour_field[0, colour_in] - link_im * colour_field[1, colour_in]
            part_im = link_re * colour_field[1, colour_in] + link_im * colour_field[0, colour_in]
            total_re = part_re if total_re is None else total_re + part_re
            total_im = part_im if total_im is None else total_im + part_im
        out_re.append(total_re)
        out_im.append(total_im)
    return jnp.stack([jnp.stack(out_re), jnp.stack(out_im)])

def displace(padded, links_block, lower_link, weights):
    centre = padded[:, :, 1:-1]
    factors = weights.astype(jnp.float32)
    fwd_x = link_times(links_block[0], jnp.roll(centre, -1, axis=4), False)
    bwd_x = jnp.roll(link_times(links_block[0], centre, True), 1, axis=4)
    fwd_y = link_times(links_block[1], jnp.roll(centre, -1, axis=3), False)
    bwd_y = jnp.roll(link_times(links_block[1], centre, True), 1, axis=3)
    fwd_z = link_times(links_block[2], padded[:, :, 2:], False)
    z_links = jnp.concatenate([lower_link[:, :, :, None], links_block[2][:, :, :, :-1]], axis=3)
    bwd_z = link_times(z_links, padded[:, :, :-2], True)
    return 0.5 * (factors[0] * (fwd_x - bwd_x) + factors[1] * (fwd_y - bwd_y) + factors[2] * (fwd_z - bwd_z))

def phase_left(vectors, momenta, zstart, ystart, zsize, ysize):
    grid_depth = vectors.shape[2]
    grid_height = vectors.shape[3]
    grid_width = vectors.shape[4]
    grid_shape = (grid_depth, grid_height, grid_width)
    zcoord = zstart + lax.broadcasted_iota(jnp.int32, grid_shape, 0)
    ycoord = ystart + lax.broadcasted_iota(jnp.int32, grid_shape, 1)
    xcoord = lax.broadcasted_iota(jnp.int32, grid_shape, 2)
    vec_re = vectors[0].astype(jnp.float32)
    vec_im = vectors[1].astype(jnp.float32)
    result = []
    for moment in range(momenta.shape[0]):
        fraction = jnp.remainder(momenta[moment, 0] * xcoord, grid_width).astype(jnp.float32) / grid_width
        fraction = fraction + jnp.remainder(momenta[moment, 1] * ycoord, ysize).astype(jnp.float32) / ysize
        fraction = fraction + jnp.remainder(momenta[moment, 2] * zcoord, zsize).astype(jnp.float32) / zsize
        phase_angle = 2.0 * math.pi * fraction
        cosine = jnp.cos(phase_angle)[None, ..., None]
        sine_part = jnp.sin(phase_angle)[None, ..., None]
        phased_re = cosine * vec_re - sine_part * vec_im
        phased_im = sine_part * vec_re + cosine * vec_im
        stacked = jnp.stack([phased_re, phased_im]).astype(jnp.bfloat16)
        result.append(stacked.reshape(-1, vectors.shape[5]))
    return jnp.stack(result)

def right_matrix(displaced):
    columns = displaced.shape[-1]
    top_rows = jnp.stack([displaced[0], displaced[1]]).reshape(-1, columns)
    bottom_rows = jnp.stack([displaced[1], -displaced[0]]).reshape(-1, columns)
    return jnp.concatenate([top_rows, bottom_rows], axis=1)

def mixing_table(perambulator, column_momentum, moment_count):
    tau_re = perambulator[0]
    tau_im = perambulator[1]
    zero_fill = jnp.zeros_like(tau_re)
    real_rows = []
    imag_rows = []
    for moment in range(moment_count):
        chosen = (column_momentum == moment)[None, :, None]
        kept_re = jnp.where(chosen, tau_re, zero_fill)
        kept_im = jnp.where(chosen, tau_im, zero_fill)
        real_rows.append(jnp.stack([kept_re, -kept_im]))
        imag_rows.append(jnp.stack([kept_im, kept_re]))
    mix_table = jnp.stack([jnp.stack(real_rows), jnp.stack(imag_rows)])
    return jnp.transpose(mix_table, (0, 3, 4, 1, 2, 5))

def unblock_vectors(blocked):
    grid = blocked.reshape(2, 3, N_SPACE // YSPLIT, YSPLIT, CZ, CY, LX, NEV)
    grid = jnp.take(grid, jnp.array([0, 1, 3, 2], dtype=jnp.int32), axis=3)
    grid = jnp.transpose(grid, (0, 1, 2, 4, 3, 5, 6, 7))
    return grid.reshape(2, 3, NZ, NY, LX, NEV)

def unblock_links(blocked):
    grid = blocked.reshape(3, 2, 3, 3, N_SPACE // YSPLIT, YSPLIT, CZ, CY, LX)
    grid = jnp.take(grid, jnp.array([0, 1, 3, 2], dtype=jnp.int32), axis=5)
    grid = jnp.transpose(grid, (0, 1, 2, 3, 4, 6, 5, 7, 8))
    return grid.reshape(3, 2, 3, 3, NZ, NY, LX)

def reference(eigvecs, links, momenta, direction, perambulator, column_momentum):
    moment_count = momenta.shape[0]
    norm_scale = 1.0 / math.sqrt(3.0 * NZ * NY * LX)
    vectors = unblock_vectors(eigvecs)
    grid_links = unblock_links(links)

    def plane_step(running, plane_index):
        neighbours = jnp.remainder(plane_index + jnp.arange(-1, 2, dtype=jnp.int32), NZ).astype(jnp.int32)
        padded = jnp.take(vectors, neighbours, axis=2).astype(jnp.float32)
        block_links = lax.dynamic_slice_in_dim(grid_links, plane_index, 1, 4).astype(jnp.float32)
        lower_index = jnp.remainder(plane_index - 1, NZ).astype(jnp.int32)
        lower_link = jnp.take(grid_links[2], lower_index, axis=3).astype(jnp.float32)
        displaced = displace(padded, block_links, lower_link, direction).astype(jnp.bfloat16)
        right_block = lax.optimization_barrier(right_matrix(displaced)).astype(jnp.float32)
        plane_vecs = lax.dynamic_slice_in_dim(vectors, plane_index, 1, 2)
        left_block = lax.optimization_barrier(phase_left(plane_vecs, momenta, plane_index, 0, NZ, NY)).astype(jnp.float32)
        elemental_term = jnp.einsum('pkn,kc->npc', left_block, right_block, precision=lax.Precision.HIGHEST)
        return (running + elemental_term.reshape(NEV, moment_count, 2, NEV), None)
    initial = jnp.zeros((NEV, moment_count, 2, NEV), jnp.float32)
    scanned = lax.scan(plane_step, initial, jnp.arange(NZ, dtype=jnp.int32))
    elementals = scanned[0] * norm_scale
    rounded = lax.optimization_barrier(elementals.astype(jnp.bfloat16)).astype(jnp.float32)
    mix_table = mixing_table(perambulator, column_momentum, moment_count).astype(jnp.float32)
    mixed_out = jnp.einsum('osjpcn,npcm->osjm', mix_table, rounded, precision=lax.Precision.HIGHEST)
    return (elementals, mixed_out)
```

```python
import math

import jax
import jax.numpy as jnp
from jax import lax
from jax.experimental import pallas as pl
from jax.experimental.pallas import tpu as pltpu
from jax.sharding import PartitionSpec as P

YSPLIT = 4


def from_behind(block, axis, distance):
    devices = range(lax.axis_size(axis))
    route = [((i - distance) % len(devices), i) for i in devices]
    return lax.ppermute(block, axis, route)


def swapped(x, axis, distance):
    return lax.ppermute(x, axis, [(i, i ^ 1 << distance) for i in range(lax.axis_size(axis))])


def link_times(links_block, colour_field, adjoint):
    out_re = []
    out_im = []
    for colour_out in range(3):
        total_re = None
        total_im = None
        for colour_in in range(3):
            if adjoint:
                link_re = links_block[0, colour_in, colour_out][..., None]
                link_im = -links_block[1, colour_in, colour_out][..., None]
            else:
                link_re = links_block[0, colour_out, colour_in][..., None]
                link_im = links_block[1, colour_out, colour_in][..., None]
            part_re = link_re * colour_field[0, colour_in] - link_im * colour_field[1, colour_in]
            part_im = link_re * colour_field[1, colour_in] + link_im * colour_field[0, colour_in]
            total_re = part_re if total_re is None else total_re + part_re
            total_im = part_im if total_im is None else total_im + part_im
        out_re.append(total_re)
        out_im.append(total_im)
    return jnp.stack([jnp.stack(out_re), jnp.stack(out_im)])


def displace_block(
    centre, z_lower, z_upper, y_lower, y_upper, links_block, zlink_lower, ylink_lower, weights
):
    factors = weights.astype(jnp.float32)
    fwd_x = link_times(links_block[0], jnp.roll(centre, -1, axis=4), False)
    bwd_x = jnp.roll(link_times(links_block[0], centre, True), 1, axis=4)
    up_y = jnp.concatenate([centre[:, :, :, 1:], y_upper[:, :, :, None]], axis=3)
    fwd_y = link_times(links_block[1], up_y, False)
    down_y = jnp.concatenate([y_lower[:, :, :, None], centre[:, :, :, :-1]], axis=3)
    ylinks_down = jnp.concatenate(
        [ylink_lower[:, :, :, :, None], links_block[1][:, :, :, :, :-1]], axis=4
    )
    bwd_y = link_times(ylinks_down, down_y, True)
    up_z = jnp.concatenate([centre[:, :, 1:], z_upper[:, :, None]], axis=2)
    fwd_z = link_times(links_block[2], up_z, False)
    down_z = jnp.concatenate([z_lower[:, :, None], centre[:, :, :-1]], axis=2)
    zlinks_down = jnp.concatenate(
        [zlink_lower[:, :, :, None], links_block[2][:, :, :, :-1]], axis=3
    )
    bwd_z = link_times(zlinks_down, down_z, True)
    return 0.5 * (
        factors[0] * (fwd_x - bwd_x) + factors[1] * (fwd_y - bwd_y) + factors[2] * (fwd_z - bwd_z)
    )


def phase_left(vectors, momenta, zstart, ystart, zsize, ysize):
    grid_depth = vectors.shape[2]
    grid_height = vectors.shape[3]
    grid_width = vectors.shape[4]
    grid_shape = (grid_depth, grid_height, grid_width)
    zcoord = zstart + lax.broadcasted_iota(jnp.int32, grid_shape, 0)
    ycoord = ystart + lax.broadcasted_iota(jnp.int32, grid_shape, 1)
    xcoord = lax.broadcasted_iota(jnp.int32, grid_shape, 2)
    vec_re = vectors[0].astype(jnp.float32)
    vec_im = vectors[1].astype(jnp.float32)
    result = []
    for moment in range(momenta.shape[0]):
        fraction = (
            jnp.remainder(momenta[moment, 0] * xcoord, grid_width).astype(jnp.float32) / grid_width
        )
        fraction = (
            fraction + jnp.remainder(momenta[moment, 1] * ycoord, ysize).astype(jnp.float32) / ysize
        )
        fraction = (
            fraction + jnp.remainder(momenta[moment, 2] * zcoord, zsize).astype(jnp.float32) / zsize
        )
        phase_angle = 2.0 * math.pi * fraction
        cosine = jnp.cos(phase_angle)[None, ..., None]
        sine_part = jnp.sin(phase_angle)[None, ..., None]
        phased_re = cosine * vec_re - sine_part * vec_im
        phased_im = sine_part * vec_re + cosine * vec_im
        stacked = jnp.stack([phased_re, phased_im]).astype(jnp.bfloat16)
        result.append(stacked.reshape(-1, vectors.shape[5]))
    return jnp.stack(result)


def right_matrix(displaced):
    columns = displaced.shape[-1]
    top_rows = jnp.stack([displaced[0], displaced[1]]).reshape(-1, columns)
    bottom_rows = jnp.stack([displaced[1], -displaced[0]]).reshape(-1, columns)
    return jnp.concatenate([top_rows, bottom_rows], axis=1)


def mixing_table(perambulator, column_momentum, moment_count):
    tau_re = perambulator[0]
    tau_im = perambulator[1]
    zero_fill = jnp.zeros_like(tau_re)
    real_rows = []
    imag_rows = []
    for moment in range(moment_count):
        chosen = (column_momentum == moment)[None, :, None]
        kept_re = jnp.where(chosen, tau_re, zero_fill)
        kept_im = jnp.where(chosen, tau_im, zero_fill)
        real_rows.append(jnp.stack([kept_re, -kept_im]))
        imag_rows.append(jnp.stack([kept_im, kept_re]))
    mix_table = jnp.stack([jnp.stack(real_rows), jnp.stack(imag_rows)])
    return jnp.transpose(mix_table, (0, 3, 4, 1, 2, 5))


def local_general(eigvecs, links, momenta, direction, perambulator, column_momentum):
    space_count = lax.axis_size("space")
    vec_count = lax.axis_size("vec")
    vectors = eigvecs[:, :, 0]
    block_links = links[:, :, :, :, 0]
    grid_depth = vectors.shape[2]
    grid_height = vectors.shape[3]
    grid_width = vectors.shape[4]
    vector_count = vectors.shape[5]
    moment_count = momenta.shape[0]
    columns = vector_count // vec_count
    owned_rows = vector_count // space_count
    z_total = grid_depth * space_count // YSPLIT
    y_total = grid_height * YSPLIT
    norm_scale = 1.0 / math.sqrt(3.0 * z_total * grid_height * YSPLIT * grid_width)
    space_index = lax.axis_index("space")
    inner_rank = space_index % YSPLIT
    y_block = jnp.bitwise_xor(inner_rank, inner_rank // 2)
    z_block = space_index // YSPLIT
    own_columns = lax.dynamic_slice_in_dim(vectors, lax.axis_index("vec") * columns, columns, 5)
    z_lower, zlink_lower = from_behind(
        (own_columns[:, :, grid_depth - 1], block_links[2, :, :, :, grid_depth - 1]),
        "space",
        YSPLIT,
    )
    z_upper = from_behind(own_columns[:, :, 0], "space", -YSPLIT)
    face_rows = (
        own_columns[:, :, :, grid_height - 1],
        block_links[1, :, :, :, :, grid_height - 1],
        own_columns[:, :, :, 0],
    )
    partner_low = swapped((face_rows[0], face_rows[1], face_rows[2]), "space", 0)
    partner_high = swapped((face_rows[0], face_rows[1], face_rows[2]), "space", 1)
    y_odd = y_block % 2 == 1
    y_lower = jnp.where(y_odd, partner_low[0], partner_high[0])
    ylink_lower = jnp.where(y_odd, partner_low[1], partner_high[1])
    y_upper = jnp.where(y_odd, partner_high[2], partner_low[2])
    displaced = displace_block(
        own_columns.astype(jnp.float32),
        z_lower.astype(jnp.float32),
        z_upper.astype(jnp.float32),
        y_lower.astype(jnp.float32),
        y_upper.astype(jnp.float32),
        block_links.astype(jnp.float32),
        zlink_lower.astype(jnp.float32),
        ylink_lower.astype(jnp.float32),
        direction,
    ).astype(jnp.bfloat16)
    right_block = right_matrix(displaced)
    phased = phase_left(
        vectors, momenta, z_block * grid_depth, y_block * grid_height, z_total, y_total
    )
    mix_table = mixing_table(perambulator, column_momentum, moment_count)
    product = jnp.einsum("pkn,kc->npc", phased, right_block, preferred_element_type=jnp.float32)
    elementals = (
        lax.psum_scatter(
            product.reshape(lax.axis_size("space") * owned_rows, moment_count, 2, columns),
            "space",
            scatter_dimension=0,
            tiled=True,
        )
        * norm_scale
    )
    rounded = elementals.astype(jnp.bfloat16)
    mixed_out = jnp.einsum(
        "osjpcn,npcm->osjm",
        mix_table,
        lax.all_gather(rounded, "space", axis=0, tiled=True),
        preferred_element_type=jnp.float32,
    )
    return (elementals, mixed_out)


LANES = 128
SUB = 8
NT = (((1,), (1,)), ((), ()))
VMEM = pl.BlockSpec(memory_space=pltpu.VMEM)
SMEM = pl.BlockSpec(memory_space=pltpu.SMEM)


def row_of(reim, out_colour, in_colour, z, depth):
    return ((reim * 3 + out_colour) * 3 + in_colour) * depth + z


def spread(row):
    return jnp.broadcast_to(row, (SUB, LANES))


def site_lanes(width):
    lane = lax.broadcasted_iota(jnp.int32, (1, LANES), 1)
    return lane % width, lane // width


def transposed(block):
    eye = (
        lax.broadcasted_iota(jnp.int32, (LANES, LANES), 0)
        == lax.broadcasted_iota(jnp.int32, (LANES, LANES), 1)
    ).astype(jnp.bfloat16)
    out = lax.dot_general(eye, block, NT, preferred_element_type=jnp.float32)
    return out.reshape(LANES // SUB, SUB, LANES)


def accumulate(total, coef, first, colour_in, value_re, value_im, z, depth):
    for colour_out in range(3):
        c_re = coef[first + row_of(0, colour_out, colour_in, z, depth)]
        c_im = coef[first + row_of(1, colour_out, colour_in, z, depth)]
        for u in range(len(value_re)):
            re = c_re * value_re[u] - c_im * value_im[u]
            im = c_re * value_im[u] + c_im * value_re[u]
            old = total[u][colour_out]
            total[u][colour_out] = (re, im) if old is None else (old[0] + re, old[1] + im)


def inner_kernel(
    depth, height, width, y_total, z_total, moments,
    momenta, direction, links, vectors, part, phases, vt, coef,
):
    columns = pl.ds(pl.multiple_of(lax.axis_index("vec") * LANES, LANES), LANES)
    tiles = LANES // SUB
    for block in range(6 * depth):
        vt[pl.ds(block * tiles, tiles)] = transposed(
            vectors[pl.ds(block * LANES, LANES), columns]
        )
    xlane, ylane = site_lanes(width)
    scaled = [
        links[k].astype(jnp.float32) * (0.5 * direction[k].astype(jnp.float32)) for k in range(3)
    ]
    x_back = jnp.where(
        xlane == 0,
        pltpu.roll(scaled[0], LANES - (width - 1), 1),
        pltpu.roll(scaled[0], 1, 1),
    )
    y_front = jnp.where(ylane == height - 1, 0.0, scaled[1])
    y_back = jnp.where(ylane == 0, 0.0, pltpu.roll(scaled[1], width, 1))
    rows = 18 * depth
    for z in range(depth):
        lower = (z - 1) % depth
        for b in range(3):
            for a in range(3):
                for reim in range(2):
                    here = row_of(reim, b, a, z, depth)
                    turned = row_of(reim, a, b, z, depth)
                    turned_low = row_of(reim, a, b, lower, depth)
                    sign = -1.0 if reim == 0 else 1.0
                    coef[here] = spread(scaled[0][here : here + 1])
                    coef[rows + here] = spread(sign * x_back[turned : turned + 1])
                    coef[2 * rows + here] = spread(y_front[here : here + 1])
                    coef[3 * rows + here] = spread(sign * y_back[turned : turned + 1])
                    coef[4 * rows + here] = spread(scaled[2][here : here + 1])
                    coef[5 * rows + here] = spread(
                        sign * scaled[2][turned_low : turned_low + 1]
                    )
    if depth == 2:
        for row in range(rows):
            coef[4 * rows + row] = coef[4 * rows + row] + coef[5 * rows + row]

    space = lax.axis_index("space")
    ystart = jnp.bitwise_xor(space, space // 2) * height
    for moment in range(moments):
        for z in range(depth):
            fraction = (
                jnp.remainder(momenta[moment, 0] * xlane, width).astype(jnp.float32) / width
                + jnp.remainder(momenta[moment, 1] * (ylane + ystart), y_total).astype(jnp.float32)
                / y_total
                + jnp.remainder(momenta[moment, 2] * (jnp.zeros_like(xlane) + z), z_total).astype(
                    jnp.float32
                )
                / z_total
            )
            angle = spread(2.0 * math.pi * fraction)
            phases[(moment * depth + z) * 2] = jnp.cos(angle)
            phases[(moment * depth + z) * 2 + 1] = jnp.sin(angle)

    first_x = xlane == 0
    last_x = xlane == width - 1
    unroll = 2
    for z in range(depth):

        def tile(step, carry):
            at = step * unroll
            total = [[None] * 3 for _ in range(unroll)]
            for a in range(3):
                re = [vt[(a * depth + z) * tiles + at + u] for u in range(unroll)]
                im = [vt[((3 + a) * depth + z) * tiles + at + u] for u in range(unroll)]

                def shifted(values, kind):
                    if kind == 0:
                        return [
                            jnp.where(
                                last_x, pltpu.roll(v, width - 1, 1), pltpu.roll(v, LANES - 1, 1)
                            )
                            for v in values
                        ]
                    if kind == 1:
                        return [
                            jnp.where(
                                first_x, pltpu.roll(v, LANES - width + 1, 1), pltpu.roll(v, 1, 1)
                            )
                            for v in values
                        ]
                    return [
                        pltpu.roll(v, LANES - width if kind == 2 else width, 1) for v in values
                    ]

                for kind in range(4):
                    accumulate(
                        total, coef, kind * rows, a, shifted(re, kind), shifted(im, kind), z, depth
                    )
                sides = (1,) if depth == 2 else (1, -1)
                for order, side in enumerate(sides):
                    other = (z + side) % depth
                    far_re = [vt[(a * depth + other) * tiles + at + u] for u in range(unroll)]
                    far_im = [vt[((3 + a) * depth + other) * tiles + at + u] for u in range(unroll)]
                    accumulate(total, coef, (4 + order) * rows, a, far_re, far_im, z, depth)
            for b in range(3):
                for u in range(unroll):
                    part[(b * depth + z) * tiles + at + u] = total[u][b][0]
                    part[((3 + b) * depth + z) * tiles + at + u] = total[u][b][1]
            return carry

        lax.fori_loop(0, tiles // unroll, tile, 0)


def outer_kernel(
    depth, height, width, moments, peers,
    direction, links, vectors, part, phases, lower, lower_links, upper,
    own, *rest,
):
    chunks = rest[:peers]
    whole = rest[peers]
    ht, coef, left, low_rows = rest[peers + 1 :]
    tiles = LANES // SUB
    for block in range(6 * depth):
        ht[pl.ds(block * tiles, tiles)] = transposed(
            jnp.concatenate(
                [
                    lower[pl.ds(block * width, width)],
                    jnp.zeros((LANES - 2 * width, LANES), jnp.bfloat16),
                    upper[pl.ds(block * width, width)],
                ],
                axis=0,
            )
        )
    _, ylane = site_lanes(width)
    scale = 0.5 * direction[1].astype(jnp.float32)
    low_rows[...] = jnp.zeros_like(low_rows)
    low_rows[:, 0:width] = lower_links[...].astype(jnp.float32) * scale
    low = low_rows[...]
    high = jnp.where(ylane == height - 1, links[1].astype(jnp.float32) * scale, 0.0)
    for z in range(depth):
        for b in range(3):
            for a in range(3):
                for reim in range(2):
                    here = row_of(reim, b, a, z, depth)
                    turned = row_of(reim, a, b, z, depth)
                    sign = -1.0 if reim == 0 else 1.0
                    coef[here] = spread(
                        high[here : here + 1] + sign * low[turned : turned + 1]
                    )
    unroll = 2
    for z in range(depth):

        def tile(step, carry):
            at = step * unroll
            total = [
                [
                    (
                        part[(b * depth + z) * tiles + at + u],
                        part[((3 + b) * depth + z) * tiles + at + u],
                    )
                    for b in range(3)
                ]
                for u in range(unroll)
            ]
            for a in range(3):
                re = [ht[(a * depth + z) * tiles + at + u] for u in range(unroll)]
                im = [ht[((3 + a) * depth + z) * tiles + at + u] for u in range(unroll)]
                accumulate(total, coef, 0, a, re, im, z, depth)
            for moment in range(moments):
                cosine = phases[(moment * depth + z) * 2]
                sine = phases[(moment * depth + z) * 2 + 1]
                for b in range(3):
                    turned_re = []
                    turned_im = []
                    for u in range(unroll):
                        re, im = total[u][b]
                        turned_re.append(cosine * re + sine * im)
                        turned_im.append(cosine * im - sine * re)
                    turned_re = jnp.concatenate(turned_re, axis=0)
                    turned_im = jnp.concatenate(turned_im, axis=0)
                    for reim in range(2):
                        span = pl.ds(((reim * 3 + b) * depth + z) * LANES, LANES)
                        row = pl.multiple_of(at * SUB, SUB * unroll)
                        real_row = pl.ds(moment * 2 * LANES + row, SUB * unroll)
                        imag_row = pl.ds((moment * 2 + 1) * LANES + row, SUB * unroll)
                        left[real_row, span] = (
                            turned_re if reim == 0 else turned_im
                        ).astype(jnp.bfloat16)
                        left[imag_row, span] = (
                            turned_im if reim == 0 else -turned_re
                        ).astype(jnp.bfloat16)
            return carry

        lax.fori_loop(0, tiles // unroll, tile, 0)
    whole[...] = jnp.dot(left[...], vectors[...], preferred_element_type=jnp.float32)
    space = lax.axis_index("space")
    own[...] = whole[:, pl.ds(pl.multiple_of(space * LANES, LANES), LANES)]
    for peer in range(peers):
        there = jnp.bitwise_xor(space, peer + 1) * LANES
        chunks[peer][...] = whole[:, pl.ds(pl.multiple_of(there, LANES), LANES)].astype(
            jnp.bfloat16
        )


def mix_kernel(moments, peers, *refs):
    whole = refs[0]
    tables = refs[1 : 2 + peers]
    chosen = refs[2 + peers : 3 + 2 * peers]
    outs = refs[3 + 2 * peers : 4 + 3 * peers]
    tau = refs[4 + 3 * peers]
    rows = tables[0].shape[0]
    half = rows // 2
    count = chosen[0].shape[0]
    for owner in range(peers + 1):
        tau[pl.ds(owner * rows, rows)] = tables[owner][...]
    products = []
    for part in range(2 * moments):
        block = whole[pl.ds(part * LANES, LANES)]
        coarse = block.astype(jnp.bfloat16)
        fine = (block - coarse.astype(jnp.float32)).astype(jnp.bfloat16)
        products.append(
            lax.dot_general(tau[...], coarse, NT, preferred_element_type=jnp.float32)
            + lax.dot_general(tau[...], fine, NT, preferred_element_type=jnp.float32)
        )
    line = lax.broadcasted_iota(jnp.int32, (half, LANES), 0) % count
    for owner in range(peers + 1):
        picked = jnp.zeros((half, LANES), jnp.int32)
        for j in range(count):
            picked = jnp.where(line == j, chosen[owner][j], picked)
        total_re = jnp.zeros((half, LANES), jnp.float32)
        total_im = jnp.zeros((half, LANES), jnp.float32)
        top = slice(owner * rows, owner * rows + half)
        bottom = slice(owner * rows + half, (owner + 1) * rows)
        for moment in range(moments):
            real, imag = products[2 * moment], products[2 * moment + 1]
            keep = picked == moment
            total_re = jnp.where(keep, real[top] - imag[bottom], total_re)
            total_im = jnp.where(keep, real[bottom] + imag[top], total_im)
        outs[owner][0:half] = total_re.astype(outs[owner].dtype)
        outs[owner][half:rows] = total_im.astype(outs[owner].dtype)


def sum_kernel(parts, peers, scale, *refs):
    own, mixed = refs[0], refs[1]
    chunks = refs[2 : 2 + peers]
    mixed_chunks = refs[2 + peers : 2 + 2 * peers]
    elementals, mixed_out = refs[2 + 2 * peers :]
    for part in range(parts):
        rows = pl.ds(part * LANES, LANES)
        total = own[rows]
        for chunk in chunks:
            total = total + chunk[rows].astype(jnp.float32)
        elementals[pl.ds(part, LANES, stride=parts)] = (total * scale).T
    total = mixed[...]
    for chunk in mixed_chunks:
        total = total + chunk[...].astype(jnp.float32)
    mixed_out[...] = total * scale


def local_fast(eigvecs, links, momenta, direction, perambulator, column_momentum):
    depth, height, width, vector_count = eigvecs.shape[3:]
    moments = momenta.shape[0]
    parts = 2 * moments
    space_count = lax.axis_size("space")
    peers = space_count - 1
    z_total = depth
    y_total = height * YSPLIT
    scale = 1.0 / math.sqrt(3.0 * z_total * y_total * width)
    ring = [g ^ (g // 2) for g in range(YSPLIT)]
    up = [(ring[g], ring[(g + 1) % YSPLIT]) for g in range(YSPLIT)]
    down = [(there, here) for here, there in up]

    def to_peer(x, peer):
        return lax.ppermute(x, "space", [(i, i ^ (peer + 1)) for i in range(space_count)])

    column = lax.axis_index("vec") * LANES
    own_columns = lax.dynamic_slice_in_dim(eigvecs[:, :, 0], column, LANES, 5)
    faces = 6 * depth * width
    lower = lax.ppermute(own_columns[:, :, :, height - 1].reshape(faces, LANES), "space", up)
    lower_links = lax.ppermute(
        links[1, :, :, :, 0, :, height - 1].reshape(18 * depth, width), "space", up
    )
    upper = lax.ppermute(own_columns[:, :, :, 0].reshape(faces, LANES), "space", down)
    rows = perambulator.shape[1] * perambulator.shape[2] * 2
    table = perambulator.reshape(rows, vector_count)
    tables = [table] + [to_peer(table, peer) for peer in range(peers)]
    chosen = [column_momentum] + [to_peer(column_momentum, peer) for peer in range(peers)]

    flat_links = links.reshape(3, 18 * depth, LANES)
    vectors = eigvecs.reshape(6 * depth * LANES, vector_count)
    tiles = 6 * depth * LANES // SUB
    part, phases = pl.pallas_call(
        lambda *refs: inner_kernel(depth, height, width, y_total, z_total, moments, *refs),
        out_shape=(
            jax.ShapeDtypeStruct((tiles, SUB, LANES), jnp.float32),
            jax.ShapeDtypeStruct((2 * moments * depth, SUB, LANES), jnp.float32),
        ),
        in_specs=[SMEM, SMEM, VMEM, VMEM],
        out_specs=(VMEM, VMEM),
        scratch_shapes=[
            pltpu.VMEM((tiles, SUB, LANES), jnp.float32),
            pltpu.VMEM((6 * 18 * depth, SUB, LANES), jnp.float32),
        ],
        cost_estimate=pl.CostEstimate(flops=80_000_000, bytes_accessed=4_000_000, transcendentals=0),
        name="inner",
    )(momenta, direction, flat_links, vectors)

    outs = pl.pallas_call(
        lambda *refs: outer_kernel(depth, height, width, moments, peers, *refs),
        out_shape=(
            jax.ShapeDtypeStruct((parts * LANES, LANES), jnp.float32),
            *[jax.ShapeDtypeStruct((parts * LANES, LANES), jnp.bfloat16)] * peers,
            jax.ShapeDtypeStruct((parts * LANES, vector_count), jnp.float32),
        ),
        in_specs=[SMEM] + [VMEM] * 7,
        out_specs=(VMEM,) * (peers + 2),
        scratch_shapes=[
            pltpu.VMEM((tiles, SUB, LANES), jnp.float32),
            pltpu.VMEM((18 * depth, SUB, LANES), jnp.float32),
            pltpu.VMEM((parts * LANES, 6 * depth * LANES), jnp.bfloat16),
            pltpu.VMEM((18 * depth, LANES), jnp.float32),
        ],
        cost_estimate=pl.CostEstimate(flops=900_000_000, bytes_accessed=4_000_000, transcendentals=0),
        name="outer",
    )(direction, flat_links, vectors, part, phases, lower, lower_links, upper)
    own, chunks, whole = outs[0], outs[1:-1], outs[-1]
    arrived = [None] * peers
    for peer in reversed(range(peers)):
        arrived[peer] = to_peer(chunks[peer], peer)

    mixed = pl.pallas_call(
        lambda *refs: mix_kernel(moments, peers, *refs),
        out_shape=(
            jax.ShapeDtypeStruct((rows, LANES), jnp.float32),
            *[jax.ShapeDtypeStruct((rows, LANES), jnp.bfloat16)] * peers,
        ),
        in_specs=[VMEM] * (2 + peers) + [SMEM] * (1 + peers),
        out_specs=(VMEM,) * (peers + 1),
        scratch_shapes=[pltpu.VMEM(((peers + 1) * rows, vector_count), jnp.bfloat16)],
        cost_estimate=pl.CostEstimate(flops=300_000_000, bytes_accessed=2_000_000, transcendentals=0),
        name="mix",
    )(whole, *tables, *chosen)
    mixed_arrived = [None] * peers
    for peer in reversed(range(peers)):
        mixed_arrived[peer] = to_peer(mixed[peer + 1], peer)

    elementals, mixed_out = pl.pallas_call(
        lambda *refs: sum_kernel(parts, peers, scale, *refs),
        out_shape=(
            jax.ShapeDtypeStruct((LANES * parts, LANES), jnp.float32),
            jax.ShapeDtypeStruct((rows, LANES), jnp.float32),
        ),
        in_specs=[VMEM] * (2 + 2 * peers),
        out_specs=(VMEM, VMEM),
        name="total",
    )(own, mixed[0], *arrived, *mixed_arrived)
    return (
        elementals.reshape(LANES, moments, 2, LANES),
        mixed_out.reshape(*perambulator.shape[:3], LANES),
    )


def local(eigvecs, *others):
    depth, height, width, vector_count = eigvecs.shape[3:]
    space_count = lax.axis_size("space")
    fits = (
        space_count == YSPLIT
        and height * width == LANES
        and vector_count == lax.axis_size("vec") * LANES
        and vector_count == space_count * LANES
    )
    return (local_fast if fits else local_general)(eigvecs, *others)


def solution(mesh):
    placed = (
        P(None, None, ("grp", "space"), None, None, None, None),
        P(None, None, None, None, ("grp", "space"), None, None, None),
        P(),
        P(),
        P(None, None, ("grp", "space"), None),
        P(("grp", "space")),
    )
    return jax.shard_map(
        local,
        mesh=mesh,
        in_specs=placed,
        out_specs=(P(("grp", "space"), None, None, "vec"), P(None, None, ("grp", "space"), "vec")),
        check_vma=False,
    )
```
